512 devices in a mesh: dom: 64 (over x, z, core), sub: 8 (over y).
Axes of the slice: x: 4, y: 8, z: 8, core: 2. Of those that a mesh axis runs over, the one named last changes fastest.
Arguments:
- node_features: bfloat16 [1048576, 128], P(('dom', 'sub')), may hold values from -6 to 6
- near_fine: int32 [8192, 3], P(('dom', 'sub')), may hold values from 0 to 8191, as said below
- near_mid: int32 [2048, 3], replicated, may hold values from 0 to 2047, as said below
- near_top: int32 [512, 3], replicated, may hold values from 0 to 511, as said below
- restrict_mid: int32 [2048, 4], replicated, may hold values from 0 to 8191, as said below
- restrict_top: int32 [512, 4], replicated, may hold values from 0 to 2047, as said below
- node_kernel: bfloat16 [3, 3, 128, 128], replicated, may hold values from -0.5 to 0.5
- channel_kernel: bfloat16 [3, 3, 128, 128], replicated, may hold values from -0.3125 to 0.3125
- restrict_weight: bfloat16 [2, 4, 128, 128], replicated, may hold values from -0.25 to 0.25
- interp_weight: bfloat16 [2, 4, 128, 128], replicated, may hold values from -0.5 to 0.5
- skip_weight: bfloat16 [128, 128], replicated, may hold values from -0.5 to 0.5
Outputs:
- updated: bfloat16 [1048576, 128], P(('dom', 'sub'))
The draws below stay inside these ranges and needn't reach their ends.
Inputs may be any that keep to these rules, and one draw needn't show every extreme that they name: `near_fine`: blocks are numbered region by region along dom+sub, 16 to a device. Row i names in column 0 a block of the same device, in column 1 one of the last 4 blocks of the previous device and in column 2 one of the first 4 blocks of the next device; where that device does not exist, a block of the same device. `near_mid`: A middle-level group is the 16 blocks numbered g * 16 to (g + 1) * 16 - 1 with g = D * 8 + s, D < 64 // 4. Row i of group (D, s) names in column 0 a block of its group, in column 1 one of the last 4 blocks of group (D - 1, s) and in column 2 one of the first 4 blocks of group (D + 1, s); where that group does not exist, a block of its own group. `near_top`: as for near_mid, with groups (D, s), D < 64 // 16, of the coarsest level. `restrict_mid`: row j = (D * 8 + s) * 16 + b lists, in some order, the four blocks ((4 D + r) * 8 + s) * 16 + b for r = 0..3 of the finest level. `restrict_top`: row j = (D * 8 + s) * 16 + b lists, in some order, the four blocks ((4 D + r) * 8 + s) * 16 + b for r = 0..3 of the middle level.
All inputs are finite; a program needn't handle non-finite values.
Results may differ from the reference program's by a relative error of at most 0.0075.
Values may be sent and summed in bfloat16 or wider, within the bound.
No kernel may reach another device: no remote copies, remote signals or barrier semaphores. Data moves between devices by JAX's collectives and lax.ppermute only.
A program may use at most 64 MiB of HBM per device.

```python
import jax
import jax.numpy as jnp

C = 128
BS = 128
KN = 3
LEVELS = 3
BLK_DEV = 16
HALO_BLK = 4
B0 = 8192
NODES = 1048576
N_DOM = 64
N_SUB = 8
DEVICES = 512


def near_pattern(key, tier_index):
    blocks_total = B0 // 4 ** tier_index
    block_ids = jnp.arange(blocks_total, dtype=jnp.int32)
    group_of = block_ids // BLK_DEV
    if tier_index == 0:
        step_groups = 1
        has_lower = group_of > 0
        has_upper = group_of < DEVICES - 1
    else:
        step_groups = N_SUB
        dom_group = group_of // N_SUB
        has_lower = dom_group > 0
        has_upper = dom_group < N_DOM // 4 ** tier_index - 1
    key_own, key_spare, key_extra, key_lower, key_upper = jax.random.split(key, 5)
    own_pick = group_of * BLK_DEV + jax.random.randint(key_own, (blocks_total,), 0, BLK_DEV, dtype=jnp.int32)
    spare_one = group_of * BLK_DEV + jax.random.randint(key_spare, (blocks_total,), 0, BLK_DEV, dtype=jnp.int32)
    spare_two = group_of * BLK_DEV + jax.random.randint(key_extra, (blocks_total,), 0, BLK_DEV, dtype=jnp.int32)
    lower_pick = (group_of - step_groups) * BLK_DEV + BLK_DEV - HALO_BLK + jax.random.randint(key_lower, (blocks_total,), 0, HALO_BLK, dtype=jnp.int32)
    upper_pick = (group_of + step_groups) * BLK_DEV + jax.random.randint(key_upper, (blocks_total,), 0, HALO_BLK, dtype=jnp.int32)
    column_one = jnp.where(has_lower, lower_pick, spare_one)
    column_two = jnp.where(has_upper, upper_pick, spare_two)
    return jnp.stack([own_pick, column_one, column_two], axis=1).astype(jnp.int32)


def child_pattern(key, tier_index):
    blocks_total = B0 // 4 ** tier_index
    block_ids = jnp.arange(blocks_total, dtype=jnp.int32)
    group_of = block_ids // BLK_DEV
    inner_pos = block_ids % BLK_DEV
    dom_group = group_of // N_SUB
    sub_part = group_of % N_SUB
    children = jnp.stack([((4 * dom_group + quarter) * N_SUB + sub_part) * BLK_DEV + inner_pos for quarter in range(4)], axis=1)
    scores = jax.random.randint(key, (blocks_total, 4), 0, 2 ** 20, dtype=jnp.int32) * 4 + jnp.arange(4, dtype=jnp.int32)
    ranking = jnp.argsort(scores, axis=1, stable=True)
    return jnp.take_along_axis(children, ranking, axis=1).astype(jnp.int32)


def draw_near_fine(key, part):
    return near_pattern(jax.random.fold_in(key, 11), 0)


def draw_near_mid(key, part):
    return near_pattern(jax.random.fold_in(key, 12), 1)


def draw_near_top(key, part):
    return near_pattern(jax.random.fold_in(key, 13), 2)


def draw_restrict_mid(key, part):
    return child_pattern(jax.random.fold_in(key, 21), 1)


def draw_restrict_top(key, part):
    return child_pattern(jax.random.fold_in(key, 22), 2)


def shard_levels(rng, extent, cuts, smallest, top_value):
    level = 1.0
    for dim, blocks in cuts:
        draws = jax.random.uniform(jax.random.fold_in(jax.random.fold_in(rng, 6), dim), (blocks,), jnp.float32, smallest / len(cuts), top_value / len(cuts))
        level = level * jnp.repeat(jnp.exp(draws), extent[dim] // blocks).reshape((-1,) + (1,) * (len(extent) - 1 - dim))
    return level


def centred(rng, dims, width, bound, shards=(), kind=jnp.bfloat16):
    entries = width * jax.random.normal(rng, dims, jnp.float32)
    if shards:
        entries = entries * shard_levels(rng, dims, shards, -0.22, 0.18)
    return jnp.clip(entries, -bound, bound).astype(kind)


def setup_inputs(seed: int = 0) -> dict:
    keys = jax.random.split(jax.random.key(seed), 12)
    node_features = centred(keys[0], (NODES, C), 1.0, 6.0, ((0, 512),))
    near_fine = draw_near_fine(jax.random.fold_in(keys[11], 71), 0)
    near_mid = draw_near_mid(jax.random.fold_in(keys[11], 71), 0)
    near_top = draw_near_top(jax.random.fold_in(keys[11], 71), 0)
    restrict_mid = draw_restrict_mid(jax.random.fold_in(keys[11], 71), 0)
    restrict_top = draw_restrict_top(jax.random.fold_in(keys[11], 71), 0)
    node_kernel = centred(keys[6], (LEVELS, KN, BS, BS), BS ** -0.5, 0.5)
    channel_kernel = centred(keys[7], (LEVELS, KN, C, C), (KN * C) ** -0.5, 0.3125)
    restrict_weight = centred(keys[8], (LEVELS - 1, 4, BS, BS), (4 * BS) ** -0.5, 0.25)
    interp_weight = centred(keys[9], (LEVELS - 1, 4, BS, BS), BS ** -0.5, 0.5)
    skip_weight = centred(keys[10], (C, C), C ** -0.5, 0.5)
    return {"node_features": node_features, "near_fine": near_fine, "near_mid": near_mid, "near_top": near_top, "restrict_mid": restrict_mid, "restrict_top": restrict_top, "node_kernel": node_kernel, "channel_kernel": channel_kernel, "restrict_weight": restrict_weight, "interp_weight": interp_weight, "skip_weight": skip_weight}


def near_level(values, near_rows, node_mats, chan_mats):
    flat_rows = values.reshape(-1, C)
    summed = jnp.zeros(values.shape, jnp.float32)
    for column in range(KN):
        mixed_rows = jnp.dot(flat_rows, chan_mats[column], preferred_element_type=jnp.float32).astype(jnp.bfloat16).reshape(values.shape)
        picked = jnp.take(mixed_rows, near_rows[:, column], axis=0)
        summed = summed + jnp.einsum("pq,bqc->bpc", node_mats[column].astype(jnp.float32), picked.astype(jnp.float32))
    return summed


def restrict_level(values, kid_rows, matrices):
    summed = jnp.zeros((kid_rows.shape[0], BS, C), jnp.float32)
    for quarter in range(4):
        picked = jnp.take(values, kid_rows[:, quarter], axis=0)
        summed = summed + jnp.einsum("pq,bqc->bpc", matrices[quarter].astype(jnp.float32), picked.astype(jnp.float32))
    return summed.astype(jnp.bfloat16)


def interp_level(coarse, kid_rows, matrices, fine_count):
    added = jnp.zeros((fine_count, BS, C), jnp.float32)
    for quarter in range(4):
        values = jnp.einsum("pq,bqc->bpc", matrices[quarter].astype(jnp.float32), coarse.astype(jnp.float32))
        added = added.at[kid_rows[:, quarter]].add(values)
    return added


def reference(node_features, near_fine, near_mid, near_top, restrict_mid, restrict_top, node_kernel, channel_kernel, restrict_weight, interp_weight, skip_weight):
    near_lists = [near_fine, near_mid, near_top]
    kid_lists = [restrict_mid, restrict_top]
    levels_values = [node_features.reshape(-1, BS, C)]
    for tier_index in range(LEVELS - 1):
        levels_values.append(restrict_level(levels_values[tier_index], kid_lists[tier_index], restrict_weight[tier_index]))
    upward = near_level(levels_values[LEVELS - 1], near_lists[LEVELS - 1], node_kernel[LEVELS - 1], channel_kernel[LEVELS - 1])
    for tier_index in range(LEVELS - 2, -1, -1):
        coarse = upward.astype(jnp.bfloat16)
        near_part = near_level(levels_values[tier_index], near_lists[tier_index], node_kernel[tier_index], channel_kernel[tier_index])
        upward = near_part + interp_level(coarse, kid_lists[tier_index], interp_weight[tier_index], levels_values[tier_index].shape[0])
    skip_term = jnp.dot(node_features, skip_weight, preferred_element_type=jnp.float32)
    return jax.nn.gelu(skip_term + upward.reshape(-1, C)).astype(jnp.bfloat16)
```

```python
import jax
import jax.numpy as jnp
from jax import lax
from jax.experimental import pallas as pl
from jax.experimental.pallas import tpu as pltpu
from jax.sharding import Mesh, PartitionSpec as P

C = 128
BS = 128
KN = 3
BLK = 16
HALO = 4
F32 = jnp.float32
BF16 = jnp.bfloat16
AXES = ("x", "r", "zl", "c", "y")
QUAD = ("zl", "c")

VMEM = pl.BlockSpec(memory_space=pltpu.VMEM)
SMEM = pl.BlockSpec(memory_space=pltpu.SMEM)


def dot(a, b):
    return jnp.dot(a, b, preferred_element_type=F32)


def call(body, out_shape, specs, flops, nbytes, **kw):
    return pl.pallas_call(
        body,
        out_shape=out_shape,
        in_specs=specs,
        out_specs=VMEM if not isinstance(out_shape, (tuple, list)) else [VMEM] * len(out_shape),
        cost_estimate=pl.CostEstimate(flops=flops, bytes_accessed=nbytes, transcendentals=0),
        **kw,
    )


def restrict_body(slot, w, own, a, b, c, out):
    parts = (own, a, b, c)
    for i in range(4):
        acc = None
        for d in range(4):
            term = dot(w[slot[4 * i + d]], parts[d][i])
            acc = term if acc is None else acc + term
        out[i] = acc.astype(BF16)


def restrict_top_body(slot, w, own, low, high, far, out):
    parts = (own, low, high, far)
    for i in range(4):
        acc = None
        for d in range(4):
            term = dot(w[slot[4 * i + d]], parts[d][i])
            acc = term if acc is None else acc + term
        out[1 + i] = acc.astype(BF16)
    out[0] = high[0]
    out[5] = low[3]


def near_pair(pos, i, win, nodes, chan):
    cols = []
    for k in range(KN):
        pair = jnp.concatenate([win[pos[3 * i + k]], win[pos[3 * i + 3 + k]]], axis=0)
        mixed = dot(pair, chan[k]).astype(BF16)
        cols.append(jnp.concatenate([mixed[:BS], mixed[BS:]], axis=1))
    return dot(nodes, jnp.concatenate(cols, axis=0))


def wide(node):
    return jnp.concatenate([node[k] for k in range(KN)], axis=1)


def fine_body(pos, win, v0, node, chan, skip, out):
    nodes = wide(node)
    for i in range(0, BLK, 2):
        near = near_pair(pos, i, win, nodes, chan)
        own = jnp.concatenate([v0[i], v0[i + 1]], axis=0)
        skipped = dot(own, skip[...])
        out[i] = near[:, :C] + skipped[:BS]
        out[i + 1] = near[:, C:] + skipped[BS:]


def upward_body(pos1, pos2, slot1, slot2, win1, win2, node1, node2, chan1, chan2, interp1, interp2, acc0, out):
    nodes1 = wide(node1)
    nodes2 = wide(node2)
    for i in range(0, BLK, 2):
        top = near_pair(pos2, i, win2, nodes2, chan2)
        mid = near_pair(pos1, i, win1, nodes1, chan1)
        for h in range(2):
            b = i + h
            lanes = slice(h * C, h * C + C)
            u1 = mid[:, lanes] + dot(interp2[slot2[b]], top[:, lanes].astype(BF16))
            u0 = acc0[b] + dot(interp1[slot1[b]], u1.astype(BF16))
            out[b] = jax.nn.gelu(u0).astype(BF16)


def slots_of(rows, shift):
    child = (rows // shift) % 4
    which = jnp.arange(4, dtype=jnp.int32)
    hit = child[:, :, None] == which[None, None, :]
    return jnp.sum(jnp.where(hit, which[None, :, None], 0), axis=1)


def places(rows, start, pitch, strided):
    rel = rows - start
    inner = (rel % 4) * 4 + rel // 4 if strided else rel
    low = rel + pitch - (BLK - HALO) + BLK
    high = rel - pitch + BLK + HALO
    pos = jnp.where(rel < 0, low, jnp.where(rel >= BLK, high, inner))
    return jnp.clip(pos, 0, BLK + 2 * HALO - 1).reshape(-1)


def shards(v, near_fine, near_mid, near_top, restrict_mid, restrict_top, node, chan, restrict_w, interp_w, skip):
    x, r, zl, c, y = (lax.axis_index(a) for a in AXES)
    nx, nr, nzl, nc, ny = (lax.axis_size(a) for a in AXES)
    q = zl * nc + c
    dom = (x * nr + r) * nzl * nc + q
    v0 = v.reshape(BLK, BS, C)
    quads = v0.reshape(4, 4, BS, C)

    def member(index):
        return lax.dynamic_index_in_dim(quads, index, axis=1, keepdims=False)

    def swap(d):
        return lax.ppermute(member(q ^ d), QUAD, [(j, j ^ d) for j in range(4)])

    got = [swap(d) for d in (1, 2, 3)]
    total = nx * nr * nzl * nc * ny
    up = [(i, i + 1) for i in range(total - 1)]
    before = lax.ppermute(v0[BLK - HALO :], AXES, up)
    after = lax.ppermute(v0[:HALO], AXES, [(j, i) for i, j in up])

    start0 = (dom * ny + y) * BLK
    start1 = ((x * nr + r) * ny + y) * BLK
    start2 = (x * ny + y) * BLK
    rows1 = lax.dynamic_slice_in_dim(restrict_mid, start1, BLK, 0)
    rows2 = lax.dynamic_slice_in_dim(restrict_top, start2, BLK, 0)
    slot1 = slots_of(rows1, ny * BLK)
    slot2 = slots_of(rows2, ny * BLK)
    pos0 = places(near_fine, start0, BLK, False)
    pos1 = places(lax.dynamic_slice_in_dim(near_mid, start1, BLK, 0), start1, ny * BLK, True)
    pos2 = places(lax.dynamic_slice_in_dim(near_top, start2, BLK, 0), start2, ny * BLK, True)

    order = jnp.arange(4, dtype=jnp.int32)

    def own_slots(slot, who):
        mine = lax.dynamic_index_in_dim(slot.reshape(4, 4, 4), q, axis=1, keepdims=False)
        hit = who[None, :, None] == order[None, None, :]
        return jnp.sum(jnp.where(hit, mine[:, None, :], 0), axis=2).reshape(-1)

    block = BS * C * 2
    v1 = call(
        restrict_body,
        jax.ShapeDtypeStruct((4, BS, C), BF16),
        [SMEM] + [VMEM] * 5,
        16 * 2 * BS * BS * C,
        24 * block,
        name="restrict_mid",
    )(own_slots(slot1, q ^ order), restrict_w[0], member(q), *got)

    low1 = lax.ppermute(v1, "r", [(i, (i + 1) % nr) for i in range(nr)])
    high1 = lax.ppermute(v1, "r", [((i + 1) % nr, i) for i in range(nr)])
    far1 = lax.ppermute(v1, "r", [(i, (i + 2) % nr) for i in range(nr)])
    all1 = lax.all_gather(v1, QUAD, axis=0, tiled=True)

    who2 = (r + jnp.array([0, 3, 1, 2], jnp.int32)) % nr
    part2 = call(
        restrict_top_body,
        jax.ShapeDtypeStruct((6, BS, C), BF16),
        [SMEM] + [VMEM] * 5,
        16 * 2 * BS * BS * C,
        26 * block,
        name="restrict_top",
    )(own_slots(slot2, who2), restrict_w[1], v1, low1, high1, far1)
    all2 = lax.all_gather(part2, QUAD, axis=0, tiled=True).reshape(4, 6, BS, C)

    xlow = lax.ppermute(all2[:, 4:6], "x", [(i, i + 1) for i in range(nx - 1)])
    xhigh = lax.ppermute(all2[:, 0:2], "x", [(i + 1, i) for i in range(nx - 1)])

    win0 = jnp.concatenate([v0, before, after], axis=0)
    acc0 = call(
        fine_body,
        jax.ShapeDtypeStruct((BLK, BS, C), F32),
        [SMEM] + [VMEM] * 5,
        7 * BLK * 2 * BS * BS * C,
        100 * block,
        name="fine",
    )(pos0, win0, v0, node[0], chan[0], skip)

    inner2 = all2[:, 1:5].reshape(BLK, BS, C)
    win2 = jnp.concatenate([inner2, xlow[:, 0], xhigh[:, 1]], axis=0)
    low = jnp.where(r == 0, xlow[:, 1], all2[:, 5])
    high = jnp.where(r == nr - 1, xhigh[:, 0], all2[:, 0])
    win1 = jnp.concatenate([all1, low, high], axis=0)

    pick1 = lax.dynamic_index_in_dim(slot1, q, axis=1, keepdims=False)
    pick2 = lax.dynamic_index_in_dim(slot2, r, axis=1, keepdims=False)
    out = call(
        upward_body,
        jax.ShapeDtypeStruct((BLK, BS, C), BF16),
        [SMEM] * 4 + [VMEM] * 9,
        14 * BLK * 2 * BS * BS * C,
        150 * block,
        name="upward",
    )(pos1, pos2, pick1, pick2, win1, win2, node[1], node[2], chan[1], chan[2], interp_w[0], interp_w[1], acc0)
    return out.reshape(BLK * BS, C)


def solution(mesh):
    names = ("dom", "sub")
    dom, sub = (mesh.shape[a] for a in names)
    grid = Mesh(mesh.devices.reshape(dom // 16, 4, 2, 2, sub), AXES)
    split = P(AXES, None)
    specs = (split, split) + (P(),) * 9
    return jax.shard_map(shards, mesh=grid, in_specs=specs, out_specs=split, check_vma=False)
```

```python
import jax
import jax.numpy as jnp
from jax import lax
from jax.experimental import pallas as pl
from jax.experimental.pallas import tpu as pltpu
from jax.sharding import Mesh, PartitionSpec as P


C = 128
BS = 128
KN = 3
BLK = 16
HALO = 4
F32 = jnp.float32
BF16 = jnp.bfloat16
I32 = jnp.int32
AXES = ("x", "r", "zl", "c", "y")
QUAD = ("zl", "c")

VMEM = pl.BlockSpec(memory_space=pltpu.VMEM)
SMEM = pl.BlockSpec(memory_space=pltpu.SMEM)

SLOT1, SLOT2, PICK1, PICK2, POS0, POS1, POS2, FLAG = 0, 16, 24, 40, 56, 104, 152, 200
LOW0, HIGH0, LOW1, HIGH1, LOW2, HIGH2, ODD, FIRST, LAST = range(FLAG, FLAG + 9)


def dot(a, b):
    return jnp.dot(a, b, preferred_element_type=F32)


def call(body, shape, dtype, n_in, products, blocks, scratch=(), limit=4, copies=1):
    made = jax.ShapeDtypeStruct(shape, dtype)
    return pl.pallas_call(
        body,
        out_shape=made if copies == 1 else [made] * copies,
        in_specs=[SMEM] + [VMEM] * n_in,
        out_specs=VMEM if copies == 1 else [VMEM] * copies,
        scratch_shapes=scratch,
        cost_estimate=pl.CostEstimate(
            flops=products * 2 * BS * BS * C, bytes_accessed=blocks * BS * C * 2, transcendentals=0
        ),
        compiler_params=pltpu.CompilerParams(vmem_limit_bytes=limit << 20),
    )


def restrict_body(tab, w, own, a, b, c, out):
    parts = (own, a, b, c)
    for i in range(4):
        acc = dot(w[0, tab[SLOT1 + 4 * i]], own[i])
        for d in range(1, 4):
            acc = acc + dot(w[0, tab[SLOT1 + 4 * i + d]], parts[d][i])
        out[i] = acc.astype(BF16)


def half_body(tab, w, own, other, out):
    for i in range(4):
        acc = dot(w[1, tab[SLOT2 + 2 * i]], own[i]) + dot(w[1, tab[SLOT2 + 2 * i + 1]], other[i])
        out[i] = acc.astype(BF16)
    out[4] = own[3 * tab[ODD]]


def join_body(tab, mine, theirs, other, out):
    for i in range(4):
        out[1 + i] = (mine[i].astype(F32) + theirs[i].astype(F32)).astype(BF16)
    odd = tab[ODD]

    @pl.when(odd == 1)
    def _():
        out[0] = theirs[4]
        out[5] = other[3]

    @pl.when(odd == 0)
    def _():
        out[0] = other[0]
        out[5] = theirs[4]


def mix(dst, at, blocks, weight):
    rows = jnp.concatenate(blocks, axis=0)
    got = dot(rows, weight).astype(BF16)
    for j in range(len(blocks)):
        dst[at + j] = got[j * BS : (j + 1) * BS]


def mix_all(dst, own, weight):
    for g in range(4):
        mix(dst, 4 * g, own(g), weight)


def mix_side(dst, own, sides, weight, present):
    for flag, blocks in sides:

        @pl.when(flag)
        def _(blocks=blocks):
            mix(dst, 0, blocks(), weight)

    @pl.when(jnp.logical_not(present))
    def _():
        mix_all(dst, own, weight)


def wide(node, level, columns):
    return jnp.concatenate([node[level, k] for k in columns], axis=1)


def near_pair(tab, at, i, mixed, nodes, columns):
    cols = []
    for k in columns:
        m = mixed[k]
        cols.append(jnp.concatenate([m[tab[at + 3 * i + k]], m[tab[at + 3 * i + 3 + k]]], axis=1))
    return dot(nodes, jnp.concatenate(cols, axis=0))


def fine_body(tab, v0, before, after, node, chan, skip, out, m0, m1, m2):
    own = lambda g: [v0[4 * g + j] for j in range(4)]
    mix_all(m0, own, chan[0, 0])
    low, high = tab[LOW0] == 1, tab[HIGH0] == 1
    mix_side(m1, own, [(low, lambda: [before[j] for j in range(4)])], chan[0, 1], low)
    mix_side(m2, own, [(high, lambda: [after[j] for j in range(4)])], chan[0, 2], high)
    nodes = wide(node, 0, range(KN))
    for i in range(0, BLK, 2):
        near = near_pair(tab, POS0, i, (m0, m1, m2), nodes, range(KN))
        skipped = dot(jnp.concatenate([v0[i], v0[i + 1]], axis=0), skip[...])
        out[i] = near[:, :C] + skipped[:BS]
        out[i + 1] = near[:, C:] + skipped[BS:]


def own_body(tab, v1, one, two, three, all2, node, chan, n1, n2, a0, b0):
    parts = (v1, one, two, three)
    mix_all(b0, lambda g: [all2[g, 1 + j] for j in range(4)], chan[2, 0])
    mix_all(a0, lambda g: [parts[g][j] for j in range(4)], chan[1, 0])
    for out, at, m, level in ((n2, POS2, b0, 2), (n1, POS1, a0, 1)):
        for i in range(0, BLK, 2):
            pair = jnp.concatenate([m[tab[at + 3 * i]], m[tab[at + 3 * i + 3]]], axis=1)
            near = dot(node[level, 0], pair)
            out[i] = near[:, :C]
            out[i + 1] = near[:, C:]


def upward_body(
    tab, v1, one, two, three, all2, xlow, xhigh, node, chan, interp, acc0, n1, n2, out, a1, a2, b1, b2
):
    parts = (v1, one, two, three)
    own2 = lambda g: [all2[g, 1 + j] for j in range(4)]
    own1 = lambda g: [parts[g][j] for j in range(4)]
    four = range(4)
    low, high = tab[LOW2] == 1, tab[HIGH2] == 1
    mix_side(b1, own2, [(low, lambda: [xlow[j, 0] for j in four])], chan[2, 1], low)
    mix_side(b2, own2, [(high, lambda: [xhigh[j, 1] for j in four])], chan[2, 2], high)
    low, high = tab[LOW1] == 1, tab[HIGH1] == 1
    first, last = tab[FIRST] == 1, tab[LAST] == 1
    mix_side(
        a1,
        own1,
        [
            (low & first, lambda: [xlow[j, 1] for j in four]),
            (low & jnp.logical_not(first), lambda: [all2[j, 5] for j in four]),
        ],
        chan[1, 1],
        low,
    )
    mix_side(
        a2,
        own1,
        [
            (high & last, lambda: [xhigh[j, 0] for j in four]),
            (high & jnp.logical_not(last), lambda: [all2[j, 0] for j in four]),
        ],
        chan[1, 2],
        high,
    )
    nodes1 = wide(node, 1, (1, 2))
    nodes2 = wide(node, 2, (1, 2))
    for i in range(0, BLK, 2):
        top = near_pair(tab, POS2, i, (None, b1, b2), nodes2, (1, 2))
        mid = near_pair(tab, POS1, i, (None, a1, a2), nodes1, (1, 2))
        for h in range(2):
            b = i + h
            lanes = slice(h * C, h * C + C)
            u2 = n2[b] + top[:, lanes]
            u1 = n1[b] + mid[:, lanes] + dot(interp[1, tab[PICK2 + b]], u2.astype(BF16))
            u0 = acc0[b] + dot(interp[0, tab[PICK1 + b]], u1.astype(BF16))
            out[b] = jax.nn.gelu(u0).astype(BF16)


def slots_of(rows, shift):
    child = (rows // shift) % 4
    which = jnp.arange(4, dtype=I32)
    hit = child[:, :, None] == which[None, None, :]
    return jnp.sum(jnp.where(hit, which[None, :, None], 0), axis=1)


def chosen(slot, who):
    hit = who[None, :, None] == jnp.arange(4, dtype=I32)[None, None, :]
    return jnp.sum(jnp.where(hit, slot[:, None, :], 0), axis=2)


def places(rows, start, pitch, key=None):
    rel = rows - start
    inner = rel if key is None else ((rel % 4) ^ key) * 4 + rel // 4
    low = rel + pitch - (BLK - HALO)
    high = rel - pitch
    pos = jnp.where(rel < 0, low, jnp.where(rel >= BLK, high, inner))
    return jnp.clip(pos, 0, BLK - 1).reshape(-1)


def body(v, near_fine, near_mid, near_top, restrict_mid, restrict_top, node, chan, restrict_w, interp_w, skip):
    x, r, zl, c, y = (lax.axis_index(a) for a in AXES)
    nx, nr, nzl, nc, ny = (lax.axis_size(a) for a in AXES)
    q = zl * nc + c
    dom = (x * nr + r) * nzl * nc + q
    v0 = v.reshape(BLK, BS, C)
    quads = v0.reshape(4, 4, BS, C)

    def member(index):
        return lax.dynamic_index_in_dim(quads, index, axis=1, keepdims=False)

    def quad_swap(value, d):
        return lax.ppermute(value, QUAD, [(j, j ^ d) for j in range(4)])

    got = [quad_swap(member(q ^ d), d) for d in (1, 2, 3)]

    total = nx * nr * nzl * nc * ny
    start0 = (dom * ny + y) * BLK
    start1 = ((x * nr + r) * ny + y) * BLK
    start2 = (x * ny + y) * BLK
    take = lax.dynamic_slice_in_dim
    slot1 = slots_of(take(restrict_mid, start1, BLK, 0), ny * BLK)
    slot2 = slots_of(take(restrict_top, start2, BLK, 0), ny * BLK)
    order = jnp.arange(4, dtype=I32)
    mine = lambda slot: lax.dynamic_index_in_dim(slot.reshape(4, 4, 4), q, axis=1, keepdims=False)
    device = (dom * ny + y, x * nr + r, x)
    ends = (total - 1, nx * nr - 1, nx - 1)
    flags = []
    for at, end in zip(device, ends):
        flags += [at > 0, at < end]
    flags += [r % 2 == 1, r == 0, r == nr - 1]
    tab = jnp.concatenate(
        [
            chosen(mine(slot1), q ^ order).reshape(-1),
            chosen(mine(slot2), r ^ order[:2]).reshape(-1),
            chosen(slot1, q[None]).reshape(-1),
            chosen(slot2, r[None]).reshape(-1),
            places(near_fine, start0, BLK),
            places(take(near_mid, start1, BLK, 0), start1, ny * BLK, q),
            places(take(near_top, start2, BLK, 0), start2, ny * BLK, 0),
            jnp.stack(flags).astype(I32),
        ]
    )

    v1 = call(restrict_body, (4, BS, C), BF16, 5, 16, 24)(tab, restrict_w, member(q), *got)

    other = lax.ppermute(v1, "r", [(j, j ^ 1) for j in range(nr)])
    rest = []
    for d in (1, 2, 3):
        rest.append(quad_swap(v1, d))

    half = call(half_body, (5, BS, C), BF16, 3, 8, 20)(tab, restrict_w, v1, other)
    theirs = lax.ppermute(half, "r", [(j, nr - 1 - j) for j in range(nr)])
    ends0, _ = lax.optimization_barrier((v0, half))
    up = [(i, i + 1) for i in range(total - 1)]
    before = lax.ppermute(ends0[BLK - HALO :], AXES, up)
    after = lax.ppermute(ends0[:HALO], AXES, [(j, i) for i, j in up])

    part2 = call(join_body, (6, BS, C), BF16, 3, 0, 18)(tab, half, theirs, other)
    all2 = lax.all_gather(part2, QUAD, axis=0, tiled=True).reshape(4, 6, BS, C)

    xlow = lax.ppermute(all2[:, 4:6], "x", [(i, i + 1) for i in range(nx - 1)])
    xhigh = lax.ppermute(all2[:, 0:2], "x", [(i + 1, i) for i in range(nx - 1)])

    mixed = pltpu.VMEM((BLK, BS, C), BF16)
    acc0 = call(fine_body, (BLK, BS, C), F32, 6, 88, 120, [mixed] * 3, 12)(
        tab, v0, before, after, node, chan, skip
    )
    n1, n2 = call(own_body, (BLK, BS, C), F32, 7, 64, 120, [mixed] * 2, 12, 2)(
        tab, v1, *rest, all2, node, chan
    )
    out = call(upward_body, (BLK, BS, C), BF16, 13, 112, 150, [mixed] * 4, 16)(
        tab, v1, *rest, all2, xlow, xhigh, node, chan, interp_w, acc0, n1, n2
    )
    return out.reshape(BLK * BS, C)


def solution(mesh):
    dom, sub = (mesh.shape[a] for a in ("dom", "sub"))
    grid = Mesh(mesh.devices.reshape(dom // 16, 4, 2, 2, sub), AXES)
    split = P(AXES, None)
    specs = (split, split) + (P(),) * 9
    return jax.shard_map(body, mesh=grid, in_specs=specs, out_specs=split, check_vma=False)
```

```python
import functools

import jax
import jax.numpy as jnp
from jax import lax
from jax.experimental import pallas as pl
from jax.experimental.pallas import tpu as pltpu
from jax.sharding import Mesh, PartitionSpec as P


C = 128
BS = 128
KN = 3
BLK = 16
HALO = 4
F32 = jnp.float32
BF16 = jnp.bfloat16
I32 = jnp.int32
AXES = ("x", "r", "zl", "c", "y")
QUAD = ("zl", "c")

VMEM = pl.BlockSpec(memory_space=pltpu.VMEM)
SMEM = pl.BlockSpec(memory_space=pltpu.SMEM)

SLOT2, PICK1, PICK2, POS0, POS1, POS2, FLAG = 0, 8, 24, 40, 88, 136, 184
LOW0, HIGH0, LOW1, HIGH1, LOW2, HIGH2, ODD, FIRST, LAST = range(FLAG, FLAG + 9)


def dot(a, b):
    return jnp.dot(a, b, preferred_element_type=F32)


def call(body, outs, products, blocks, scratch=(), limit=4):
    many = isinstance(outs, list)
    made = [jax.ShapeDtypeStruct(*o) for o in (outs if many else [outs])]

    def run(*args):
        return pl.pallas_call(
            body,
            out_shape=made if many else made[0],
            in_specs=[SMEM if a.dtype == I32 else VMEM for a in args],
            out_specs=[VMEM] * len(made) if many else VMEM,
            scratch_shapes=scratch,
            cost_estimate=pl.CostEstimate(
                flops=products * 2 * BS * BS * C, bytes_accessed=blocks * BS * C * 2, transcendentals=0
            ),
            compiler_params=pltpu.CompilerParams(vmem_limit_bytes=limit << 20),
        )(*args)

    return run


def pair_body(shift, raw, w, own, other, keep, send):
    q = raw[4 * BLK]
    zl, c = q // 2, q % 2

    def slot(b, child):
        got = 0
        for t in range(1, 4):
            kid = jnp.bitwise_and(jnp.right_shift(raw[4 * b + t], shift), 3)
            got = got + jnp.where(kid == child, t, 0)
        return got

    for out, z in ((send, 1 - zl), (keep, zl)):
        for i in range(4):
            b = 4 * i + 2 * z + c
            acc = dot(w[0, slot(b, q)], own[i, z]) + dot(w[0, slot(b, jnp.bitwise_xor(q, 1))], other[i, z])
            out[i] = acc.astype(out.dtype)


def sum_body(keep, got, out):
    for i in range(4):
        out[i] = (keep[i] + got[i].astype(F32)).astype(BF16)


def half_body(tab, w, own, other, across, keep, send, both):
    for i in range(4):
        acc = dot(w[1, tab[SLOT2 + 2 * i]], own[i]) + dot(w[1, tab[SLOT2 + 2 * i + 1]], other[i])
        keep[i] = acc
        send[i] = acc.astype(BF16)
        both[i] = own[i]
        both[4 + i] = across[i]
    send[4] = own[3 * tab[ODD]]


def join_body(odd, mine, theirs, other, out):
    for i in range(4):
        out[1 + i] = (mine[i] + theirs[i].astype(F32)).astype(BF16)
    is_odd = jnp.broadcast_to(odd[...], (BS, C)) > 0
    out[0] = jnp.where(is_odd, theirs[4], other[0])
    out[5] = jnp.where(is_odd, other[3], theirs[4])


def mix(dst, at, blocks, weight):
    rows = jnp.concatenate(blocks, axis=0)
    got = dot(rows, weight).astype(BF16)
    for j in range(len(blocks)):
        dst[at + j] = got[j * BS : (j + 1) * BS]


def mix_all(dst, own, weight):
    for g in range(4):
        mix(dst, 4 * g, own(g), weight)


def mix_side(dst, own, sides, weight, present):
    for flag, blocks in sides:

        @pl.when(flag)
        def _(blocks=blocks):
            mix(dst, 0, blocks(), weight)

    @pl.when(jnp.logical_not(present))
    def _():
        mix_all(dst, own, weight)


def wide(node, level, columns):
    return jnp.concatenate([node[level, k] for k in columns], axis=1)


def near_pair(tab, at, i, mixed, nodes, columns):
    cols = []
    for k in columns:
        m = mixed[k]
        cols.append(jnp.concatenate([m[tab[at + 3 * i + k]], m[tab[at + 3 * i + 3 + k]]], axis=1))
    return dot(nodes, jnp.concatenate(cols, axis=0))


def fine_body(tab, v0, before, after, node, chan, skip, out, m0, m1, m2):
    own = lambda g: [v0[4 * g + j] for j in range(4)]
    mix_all(m0, own, chan[0, 0])
    low, high = tab[LOW0] == 1, tab[HIGH0] == 1
    mix_side(m1, own, [(low, lambda: [before[j] for j in range(4)])], chan[0, 1], low)
    mix_side(m2, own, [(high, lambda: [after[j] for j in range(4)])], chan[0, 2], high)
    nodes = wide(node, 0, range(KN))
    for i in range(0, BLK, 2):
        near = near_pair(tab, POS0, i, (m0, m1, m2), nodes, range(KN))
        skipped = dot(jnp.concatenate([v0[i], v0[i + 1]], axis=0), skip[...])
        out[i] = near[:, :C] + skipped[:BS]
        out[i + 1] = near[:, C:] + skipped[BS:]


def quad_parts(both, core):
    return lambda d: [(core if d % 2 else both)[4 * (d // 2) + j] for j in range(4)]


def own_body(tab, both, core, all2, node, chan, n1, n2, a0, b0):
    own1 = quad_parts(both, core)
    mix_all(b0, lambda g: [all2[g, 1 + j] for j in range(4)], chan[2, 0])
    mix_all(a0, own1, chan[1, 0])
    for out, at, m, level in ((n2, POS2, b0, 2), (n1, POS1, a0, 1)):
        for i in range(0, BLK, 2):
            pair = jnp.concatenate([m[tab[at + 3 * i]], m[tab[at + 3 * i + 3]]], axis=1)
            near = dot(node[level, 0], pair)
            out[i] = near[:, :C]
            out[i + 1] = near[:, C:]


def upward_body(
    tab, both, core, all2, xlow, xhigh, node, chan, interp, acc0, n1, n2, out, a1, a2, b1, b2
):
    own2 = lambda g: [all2[g, 1 + j] for j in range(4)]
    own1 = quad_parts(both, core)
    four = range(4)
    low, high = tab[LOW2] == 1, tab[HIGH2] == 1
    mix_side(b1, own2, [(low, lambda: [xlow[j, 0] for j in four])], chan[2, 1], low)
    mix_side(b2, own2, [(high, lambda: [xhigh[j, 1] for j in four])], chan[2, 2], high)
    low, high = tab[LOW1] == 1, tab[HIGH1] == 1
    first, last = tab[FIRST] == 1, tab[LAST] == 1
    mix_side(
        a1,
        own1,
        [
            (low & first, lambda: [xlow[j, 1] for j in four]),
            (low & jnp.logical_not(first), lambda: [all2[j, 5] for j in four]),
        ],
        chan[1, 1],
        low,
    )
    mix_side(
        a2,
        own1,
        [
            (high & last, lambda: [xhigh[j, 0] for j in four]),
            (high & jnp.logical_not(last), lambda: [all2[j, 0] for j in four]),
        ],
        chan[1, 2],
        high,
    )
    nodes1 = wide(node, 1, (1, 2))
    nodes2 = wide(node, 2, (1, 2))
    for i in range(0, BLK, 2):
        top = near_pair(tab, POS2, i, (None, b1, b2), nodes2, (1, 2))
        mid = near_pair(tab, POS1, i, (None, a1, a2), nodes1, (1, 2))
        for h in range(2):
            b = i + h
            lanes = slice(h * C, h * C + C)
            u2 = n2[b] + top[:, lanes]
            u1 = n1[b] + mid[:, lanes] + dot(interp[1, tab[PICK2 + b]], u2.astype(BF16))
            u0 = acc0[b] + dot(interp[0, tab[PICK1 + b]], u1.astype(BF16))
            out[b] = jax.nn.gelu(u0).astype(BF16)


def slots_of(rows, shift):
    child = (rows // shift) % 4
    which = jnp.arange(4, dtype=I32)
    hit = child[:, :, None] == which[None, None, :]
    return jnp.sum(jnp.where(hit, which[None, :, None], 0), axis=1)


def chosen(slot, who):
    hit = who[None, :, None] == jnp.arange(4, dtype=I32)[None, None, :]
    return jnp.sum(jnp.where(hit, slot[:, None, :], 0), axis=2)


def places(rows, start, pitch, key=None):
    rel = rows - start
    inner = rel if key is None else ((rel % 4) ^ key) * 4 + rel // 4
    low = rel + pitch - (BLK - HALO)
    high = rel - pitch
    pos = jnp.where(rel < 0, low, jnp.where(rel >= BLK, high, inner))
    return jnp.clip(pos, 0, BLK - 1).reshape(-1)


def body(v, near_fine, near_mid, near_top, restrict_mid, restrict_top, node, chan, restrict_w, interp_w, skip):
    x, r, zl, c, y = (lax.axis_index(a) for a in AXES)
    nx, nr, nzl, nc, ny = (lax.axis_size(a) for a in AXES)
    q = zl * nc + c
    dom = (x * nr + r) * nzl * nc + q
    v0 = v.reshape(BLK, BS, C)
    quads = v0.reshape(4, 2, 2, BS, C)
    take = lax.dynamic_slice_in_dim
    member = lambda index: lax.dynamic_index_in_dim(quads, index, axis=2, keepdims=False)
    flip = [(0, 1), (1, 0)]

    partner = lax.ppermute(member(1 - c), "c", flip)

    total = nx * nr * nzl * nc * ny
    start0 = (dom * ny + y) * BLK
    start1 = ((x * nr + r) * ny + y) * BLK
    start2 = (x * ny + y) * BLK
    rows1 = take(restrict_mid, start1, BLK, 0)
    raw = jnp.concatenate([rows1.reshape(-1), q[None]])
    four = (4, BS, C)
    kept, sent = call(functools.partial(pair_body, (ny * BLK).bit_length() - 1), [(four, F32), (four, BF16)], 16, 40)(
        raw, restrict_w, member(c), partner
    )
    crossed = lax.ppermute(sent, "zl", flip)
    near_fine, near_mid, near_top, restrict_top, rows1, _ = lax.optimization_barrier(
        (near_fine, near_mid, near_top, restrict_top, rows1, sent)
    )
    slot1 = slots_of(rows1, ny * BLK)
    slot2 = slots_of(take(restrict_top, start2, BLK, 0), ny * BLK)
    order = jnp.arange(4, dtype=I32)
    mine = lambda slot: lax.dynamic_index_in_dim(slot.reshape(4, 4, 4), q, axis=1, keepdims=False)
    device = (dom * ny + y, x * nr + r, x)
    ends = (total - 1, nx * nr - 1, nx - 1)
    flags = []
    for at, end in zip(device, ends):
        flags += [at > 0, at < end]
    flags += [r % 2 == 1, r == 0, r == nr - 1]
    tab = jnp.concatenate(
        [
            chosen(mine(slot2), r ^ order[:2]).reshape(-1),
            chosen(slot1, q[None]).reshape(-1),
            chosen(slot2, r[None]).reshape(-1),
            places(near_fine, start0, BLK),
            places(take(near_mid, start1, BLK, 0), start1, ny * BLK, q),
            places(take(near_top, start2, BLK, 0), start2, ny * BLK, 0),
            jnp.stack(flags).astype(I32),
        ]
    )

    v1 = call(sum_body, (four, BF16), 0, 16)(kept, crossed)

    other = lax.ppermute(v1, "r", [(j, j ^ 1) for j in range(nr)])
    across = lax.ppermute(v1, "zl", flip)

    half, send, both = call(
        half_body, [(four, F32), ((5, BS, C), BF16), ((8, BS, C), BF16)], 8, 40
    )(tab, restrict_w, v1, other, across)
    theirs = lax.ppermute(send, "r", [(j, nr - 1 - j) for j in range(nr)])
    core = lax.ppermute(both, "c", flip)
    ends0, _ = lax.optimization_barrier((v0, v1))
    up = [(i, i + 1) for i in range(total - 1)]
    before = lax.ppermute(ends0[BLK - HALO :], AXES, up)
    after = lax.ppermute(ends0[:HALO], AXES, [(j, i) for i, j in up])

    odd = jnp.full((1, C), r % 2, F32)
    part2 = call(join_body, ((6, BS, C), BF16), 0, 18)(odd, half, theirs, other)
    all2 = lax.all_gather(part2, QUAD, axis=0, tiled=True).reshape(4, 6, BS, C)

    xlow = lax.ppermute(all2[:, 4:6], "x", [(i, i + 1) for i in range(nx - 1)])
    xhigh = lax.ppermute(all2[:, 0:2], "x", [(i + 1, i) for i in range(nx - 1)])

    mixed = pltpu.VMEM((BLK, BS, C), BF16)
    acc0 = call(fine_body, (v0.shape, F32), 88, 120, [mixed] * 3, 12)(
        tab, v0, before, after, node, chan, skip
    )
    n1, n2 = call(own_body, [(v0.shape, F32)] * 2, 64, 120, [mixed] * 2, 12)(
        tab, both, core, all2, node, chan
    )
    out = call(upward_body, (v0.shape, BF16), 112, 150, [mixed] * 4, 16)(
        tab, both, core, all2, xlow, xhigh, node, chan, interp_w, acc0, n1, n2
    )
    return out.reshape(BLK * BS, C)


def solution(mesh):
    dom, sub = (mesh.shape[a] for a in ("dom", "sub"))
    grid = Mesh(mesh.devices.reshape(dom // 16, 4, 2, 2, sub), AXES)
    split = P(AXES, None)
    specs = (split, split) + (P(),) * 9
    return jax.shard_map(body, mesh=grid, in_specs=specs, out_specs=split, check_vma=False)
```

```python
import functools

import jax
import jax.numpy as jnp
from jax import lax
from jax.experimental import pallas as pl
from jax.experimental.pallas import tpu as pltpu
from jax.sharding import Mesh, PartitionSpec as P


C = 128
BS = 128
KN = 3
BLK = 16
HALO = 4
F32 = jnp.float32
BF16 = jnp.bfloat16
I32 = jnp.int32
AXES = ("x", "r", "zl", "c", "y")
QUAD = ("zl", "c")

VMEM = pl.BlockSpec(memory_space=pltpu.VMEM)
SMEM = pl.BlockSpec(memory_space=pltpu.SMEM)
ANY = pl.BlockSpec(memory_space=pl.ANY)

SLOT2, PICK1, PICK2, POS0, POS1, POS2, FLAG = 0, 8, 24, 40, 88, 136, 184
LOW0, HIGH0, LOW1, HIGH1, LOW2, HIGH2 = range(FLAG, FLAG + 6)
TABLE = 256


def dot(a, b):
    return jnp.dot(a, b, preferred_element_type=F32)


def call(body, outs, products, blocks, scratch=None, limit=4):
    many = isinstance(outs, list)
    made = [jax.ShapeDtypeStruct(*o) for o in (outs if many else [outs])]

    def run(*args):
        return pl.pallas_call(
            body,
            out_shape=made if many else made[0],
            in_specs=[VMEM if a.dtype != I32 else SMEM if scratch is None else ANY for a in args],
            out_specs=[VMEM] * len(made) if many else VMEM,
            scratch_shapes=[] if scratch is None else [*scratch, pltpu.SMEM((TABLE,), I32), pltpu.SemaphoreType.DMA],
            cost_estimate=pl.CostEstimate(
                flops=products * 2 * BS * BS * C, bytes_accessed=blocks * BS * C * 2, transcendentals=0
            ),
            compiler_params=pltpu.CompilerParams(vmem_limit_bytes=limit << 20),
        )(*args)

    return run


def pair_body(shift, raw, w, own, other, keep, send):
    q = raw[4 * BLK]
    zl, c = q // 2, q % 2

    def slot(b, child):
        got = 0
        for t in range(1, 4):
            kid = jnp.bitwise_and(jnp.right_shift(raw[4 * b + t], shift), 3)
            got = got + jnp.where(kid == child, t, 0)
        return got

    for out, z in ((send, 1 - zl), (keep, zl)):
        for i in range(4):
            b = 4 * i + 2 * z + c
            acc = dot(w[0, slot(b, q)], own[i, z]) + dot(w[0, slot(b, jnp.bitwise_xor(q, 1))], other[i, z])
            out[i] = acc.astype(out.dtype)


def sum_body(keep, got, out):
    for i in range(4):
        out[i] = (keep[i] + got[i].astype(F32)).astype(BF16)


def prep_body(tab, w, own, part, chosen):
    for i in range(4):
        part[i] = dot(w[1, tab[SLOT2 + 2 * i]], own[i])
        chosen[i] = w[1, tab[SLOT2 + 2 * i + 1]]


def half_body(odd, part, chosen, own, other, across, keep, send, both):
    for i in range(4):
        acc = part[i] + dot(chosen[i], other[i])
        keep[i] = acc
        send[i] = acc.astype(BF16)
        both[i] = own[i]
        both[4 + i] = across[i]
    send[4] = jnp.where(jnp.broadcast_to(odd[...], (BS, C)) > 0, own[3], own[0])


def join_body(odd, end, mine, theirs, other, edge, out):
    for i in range(4):
        out[1 + i] = (mine[i] + theirs[i].astype(F32)).astype(BF16)
    is_odd = jnp.broadcast_to(odd[...], (BS, C)) > 0
    is_end = jnp.broadcast_to(end[...], (BS, C)) > 0
    third = jnp.where(is_end, edge[0], theirs[4])
    out[0] = jnp.where(is_odd, third, other[0])
    out[5] = jnp.where(is_odd, other[3], third)


def mix(dst, at, blocks, weight):
    rows = jnp.concatenate(blocks, axis=0)
    got = dot(rows, weight).astype(BF16)
    for j in range(len(blocks)):
        dst[at + j] = got[j * BS : (j + 1) * BS]


def mix_all(dst, own, weight):
    for g in range(4):
        mix(dst, 4 * g, own(g), weight)


def mix_absent(absent, dst, own, weight):
    @pl.when(absent)
    def _():
        mix_all(dst, own, weight)


def wide(node, level, columns):
    return jnp.concatenate([node[level, k] for k in columns], axis=1)


def near_pair(tab, at, i, mixed, nodes, columns):
    cols = []
    for k in columns:
        m = mixed[k]
        cols.append(jnp.concatenate([m[tab[at + 3 * i + k]], m[tab[at + 3 * i + 3 + k]]], axis=1))
    return dot(nodes, jnp.concatenate(cols, axis=0))


def fine_body(table, v0, before, after, node, chan, skip, out, m0, m1, m2, tab, sem):
    copy = pltpu.make_async_copy(table, tab, sem)
    copy.start()
    own = lambda g: [v0[4 * g + j] for j in range(4)]
    mix_all(m0, own, chan[0, 0])
    mix(m1, 0, [before[j] for j in range(4)], chan[0, 1])
    mix(m2, 0, [after[j] for j in range(4)], chan[0, 2])
    copy.wait()
    mix_absent(tab[LOW0] == 0, m1, own, chan[0, 1])
    mix_absent(tab[HIGH0] == 0, m2, own, chan[0, 2])
    nodes = wide(node, 0, range(KN))
    for i in range(0, BLK, 2):
        near = near_pair(tab, POS0, i, (m0, m1, m2), nodes, range(KN))
        skipped = dot(jnp.concatenate([v0[i], v0[i + 1]], axis=0), skip[...])
        out[i] = near[:, :C] + skipped[:BS]
        out[i + 1] = near[:, C:] + skipped[BS:]


def quad_parts(both, core):
    return lambda d: [(core if d % 2 else both)[4 * (d // 2) + j] for j in range(4)]


def own_body(table, both, core, all2, node, chan, n1, n2, a0, b0, tab, sem):
    copy = pltpu.make_async_copy(table, tab, sem)
    copy.start()
    mix_all(b0, lambda g: [all2[g, 1 + j] for j in range(4)], chan[2, 0])
    mix_all(a0, quad_parts(both, core), chan[1, 0])
    copy.wait()
    for out, at, m, level in ((n2, POS2, b0, 2), (n1, POS1, a0, 1)):
        for i in range(0, BLK, 2):
            pair = jnp.concatenate([m[tab[at + 3 * i]], m[tab[at + 3 * i + 3]]], axis=1)
            near = dot(node[level, 0], pair)
            out[i] = near[:, :C]
            out[i + 1] = near[:, C:]


def upward_body(
    table, both, core, all2, xlow, xhigh, node, chan, interp, acc0, n1, n2, out, a1, a2, b1, b2, c1, c2, tab, sem
):
    copy = pltpu.make_async_copy(table, tab, sem)
    copy.start()
    mix(b1, 0, [xlow[j] for j in range(4)], chan[2, 1])
    mix(b2, 0, [xhigh[j] for j in range(4)], chan[2, 2])
    mix(a1, 0, [all2[j, 5] for j in range(4)], chan[1, 1])
    mix(a2, 0, [all2[j, 0] for j in range(4)], chan[1, 2])
    copy.wait()
    own2 = lambda g: [all2[g, 1 + j] for j in range(4)]
    own1 = quad_parts(both, core)
    mix_absent(tab[LOW2] == 0, b1, own2, chan[2, 1])
    mix_absent(tab[HIGH2] == 0, b2, own2, chan[2, 2])
    mix_absent(tab[LOW1] == 0, a1, own1, chan[1, 1])
    mix_absent(tab[HIGH1] == 0, a2, own1, chan[1, 2])
    halves = (slice(0, C), slice(C, 2 * C))
    nodes2 = wide(node, 2, (1, 2))
    for i in range(0, BLK, 2):
        top = near_pair(tab, POS2, i, (None, b1, b2), nodes2, (1, 2))
        for h in range(2):
            c2[i + h] = (n2[i + h] + top[:, halves[h]]).astype(BF16)
    nodes1 = wide(node, 1, (1, 2))
    for i in range(0, BLK, 2):
        mid = near_pair(tab, POS1, i, (None, a1, a2), nodes1, (1, 2))
        for h in range(2):
            b = i + h
            c1[b] = (n1[b] + mid[:, halves[h]] + dot(interp[1, tab[PICK2 + b]], c2[b])).astype(BF16)
    for b in range(BLK):
        u0 = acc0[b] + dot(interp[0, tab[PICK1 + b]], c1[b])
        out[b] = jax.nn.gelu(u0).astype(BF16)


def slots_of(rows, shift):
    child = (rows // shift) % 4
    which = jnp.arange(4, dtype=I32)
    hit = child[:, :, None] == which[None, None, :]
    return jnp.sum(jnp.where(hit, which[None, :, None], 0), axis=1)


def chosen(slot, who):
    hit = who[None, :, None] == jnp.arange(4, dtype=I32)[None, None, :]
    return jnp.sum(jnp.where(hit, slot[:, None, :], 0), axis=2)


def places(rows, start, pitch, key=None):
    rel = rows - start
    inner = rel if key is None else ((rel % 4) ^ key) * 4 + rel // 4
    low = rel + pitch - (BLK - HALO)
    high = rel - pitch
    pos = jnp.where(rel < 0, low, jnp.where(rel >= BLK, high, inner))
    return jnp.clip(pos, 0, BLK - 1).reshape(-1)


def body(v, near_fine, near_mid, near_top, restrict_mid, restrict_top, node, chan, restrict_w, interp_w, skip):
    x, r, zl, c, y = (lax.axis_index(a) for a in AXES)
    nx, nr, nzl, nc, ny = (lax.axis_size(a) for a in AXES)
    q = zl * nc + c
    dom = (x * nr + r) * nzl * nc + q
    v0 = v.reshape(BLK, BS, C)
    quads = v0.reshape(4, 2, 2, BS, C)
    take = lax.dynamic_slice_in_dim
    member = lambda index: lax.dynamic_index_in_dim(quads, index, axis=2, keepdims=False)
    flip = [(0, 1), (1, 0)]

    partner = lax.ppermute(member(1 - c), "c", flip)

    total = nx * nr * nzl * nc * ny
    start0 = (dom * ny + y) * BLK
    start1 = ((x * nr + r) * ny + y) * BLK
    start2 = (x * ny + y) * BLK
    rows1 = take(restrict_mid, start1, BLK, 0)
    raw = jnp.concatenate([rows1.reshape(-1), q[None]])
    four = (4, BS, C)
    kept, sent = call(functools.partial(pair_body, (ny * BLK).bit_length() - 1), [(four, F32), (four, BF16)], 16, 40)(
        raw, restrict_w, member(c), partner
    )
    crossed = lax.ppermute(sent, "zl", flip)
    near_fine, near_mid, near_top, restrict_top, rows1, _ = lax.optimization_barrier(
        (near_fine, near_mid, near_top, restrict_top, rows1, sent)
    )
    slot1 = slots_of(rows1, ny * BLK)
    slot2 = slots_of(take(restrict_top, start2, BLK, 0), ny * BLK)
    order = jnp.arange(4, dtype=I32)
    mine = lambda slot: lax.dynamic_index_in_dim(slot.reshape(4, 4, 4), q, axis=1, keepdims=False)
    device = (dom * ny + y, x * nr + r, x)
    ends = (total - 1, nx * nr - 1, nx - 1)
    flags = []
    for at, end in zip(device, ends):
        flags += [at > 0, at < end]
    tab = jnp.concatenate(
        [
            chosen(mine(slot2), r ^ order[:2]).reshape(-1),
            chosen(slot1, q[None]).reshape(-1),
            chosen(slot2, r[None]).reshape(-1),
            places(near_fine, start0, BLK),
            places(take(near_mid, start1, BLK, 0), start1, ny * BLK, q),
            places(take(near_top, start2, BLK, 0), start2, ny * BLK, 0),
            jnp.stack(flags).astype(I32),
            jnp.zeros((TABLE - FLAG - 6,), I32),
        ]
    )

    v1 = call(sum_body, (four, BF16), 0, 16)(kept, crossed)

    other = lax.ppermute(v1, "r", [(j, j ^ 1) for j in range(nr)])
    across = lax.ppermute(v1, "zl", flip)

    part, chosen2 = call(prep_body, [(four, F32), (four, BF16)], 4, 20)(tab, restrict_w, v1)
    odd = jnp.full((1, C), r % 2, F32)
    end = jnp.full((1, C), (r == 0) | (r == nr - 1), F32)
    half, send, both = call(
        half_body, [(four, F32), ((5, BS, C), BF16), ((8, BS, C), BF16)], 4, 40
    )(odd, part, chosen2, v1, other, across)
    theirs = lax.ppermute(send, "r", [(j, nr - 1 - j) for j in range(nr)])
    late1, _ = lax.optimization_barrier((v1, send))
    hop = [(nr * (i + 1) - 1, nr * (i + 1)) for i in range(nx - 1)]
    edge = lax.ppermute(
        jnp.where(r == 0, late1[:1], late1[3:]), ("x", "r"), hop + [(j, i) for i, j in hop]
    )
    core = lax.ppermute(both, "c", flip)
    ends0, _ = lax.optimization_barrier((v0, v1))
    up = [(i, i + 1) for i in range(total - 1)]
    before = lax.ppermute(ends0[BLK - HALO :], AXES, up)
    after = lax.ppermute(ends0[:HALO], AXES, [(j, i) for i, j in up])

    part2 = call(join_body, ((6, BS, C), BF16), 0, 18)(odd, end, half, theirs, other, edge)
    all2 = lax.all_gather(part2, QUAD, axis=0, tiled=True).reshape(4, 6, BS, C)

    xlow = lax.ppermute(all2[:, 4], "x", [(i, i + 1) for i in range(nx - 1)])
    xhigh = lax.ppermute(all2[:, 1], "x", [(i + 1, i) for i in range(nx - 1)])

    mixed = pltpu.VMEM((BLK, BS, C), BF16)
    acc0 = call(fine_body, (v0.shape, F32), 88, 120, [mixed] * 3, 12)(
        tab, v0, before, after, node, chan, skip
    )
    n1, n2 = call(own_body, [(v0.shape, F32)] * 2, 64, 120, [mixed] * 2, 12)(
        tab, both, core, all2, node, chan
    )
    out = call(upward_body, (v0.shape, BF16), 112, 150, [mixed] * 6, 16)(
        tab, both, core, all2, xlow, xhigh, node, chan, interp_w, acc0, n1, n2
    )
    return out.reshape(BLK * BS, C)


def solution(mesh):
    dom, sub = (mesh.shape[a] for a in ("dom", "sub"))
    grid = Mesh(mesh.devices.reshape(dom // 16, 4, 2, 2, sub), AXES)
    split = P(AXES, None)
    specs = (split, split) + (P(),) * 9
    return jax.shard_map(body, mesh=grid, in_specs=specs, out_specs=split, check_vma=False)
```

```python
import functools

import jax
import jax.numpy as jnp
from jax import lax
from jax.experimental import pallas as pl
from jax.experimental.pallas import tpu as pltpu
from jax.sharding import Mesh, PartitionSpec as P


C = 128
BS = 128
KN = 3
BLK = 16
HALO = 4
F32 = jnp.float32
BF16 = jnp.bfloat16
I32 = jnp.int32
AXES = ("x", "r", "zl", "c", "y")
QUAD = ("zl", "c")

VMEM = pl.BlockSpec(memory_space=pltpu.VMEM)
SMEM = pl.BlockSpec(memory_space=pltpu.SMEM)
ANY = pl.BlockSpec(memory_space=pl.ANY)

PICK1, PICK2, POS0, POS1, POS2, FLAG = 0, 16, 32, 80, 128, 176
LOW0, HIGH0, LOW1, HIGH1, LOW2, HIGH2 = range(FLAG, FLAG + 6)
TABLE = 256


def dot(a, b):
    return jnp.dot(a, b, preferred_element_type=F32)


def call(body, outs, products, blocks, scratch=None, limit=4):
    many = isinstance(outs, list)
    made = [jax.ShapeDtypeStruct(*o) for o in (outs if many else [outs])]

    def run(*args):
        return pl.pallas_call(
            body,
            out_shape=made if many else made[0],
            in_specs=[VMEM if a.dtype != I32 else SMEM if scratch is None else ANY for a in args],
            out_specs=[VMEM] * len(made) if many else VMEM,
            scratch_shapes=[] if scratch is None else [*scratch, pltpu.SMEM((TABLE,), I32), pltpu.SemaphoreType.DMA],
            cost_estimate=pl.CostEstimate(
                flops=products * 2 * BS * BS * C, bytes_accessed=blocks * BS * C * 2, transcendentals=0
            ),
            compiler_params=pltpu.CompilerParams(vmem_limit_bytes=limit << 20),
        )(*args)

    return run


def pair_body(shift, raw, w, own, gifts, keep, send):
    q = raw[4 * BLK]
    zl, c = q // 2, q % 2

    def slot(b, child):
        got = 0
        for t in range(1, 4):
            kid = jnp.bitwise_and(jnp.right_shift(raw[4 * b + t], shift), 3)
            got = got + jnp.where(kid == child, t, 0)
        return got

    for out, z in ((send, 1 - zl), (keep, zl)):
        for i in range(4):
            b = 4 * i + 2 * z + c
            acc = dot(w[0, slot(b, q)], own[i, z, c]) + dot(w[0, slot(b, jnp.bitwise_xor(q, 1))], gifts[1 - c, i, z])
            out[i] = acc.astype(out.dtype)


def sum_body(keep, got, out):
    for i in range(4):
        out[i] = (keep[i] + got[i].astype(F32)).astype(BF16)


def choose_body(slot, w, chosen):
    for i in range(8):
        chosen[i] = w[1, slot[i]]


def half_body(odd, chosen, own, other, keep, send):
    for i in range(4):
        acc = dot(chosen[2 * i], own[i]) + dot(chosen[2 * i + 1], other[i])
        keep[i] = acc
        send[i] = acc.astype(BF16)
    send[4] = jnp.where(jnp.broadcast_to(odd[...], (BS, C)) > 0, own[3], own[0])


def join_body(odd, end, mine, theirs, other, edge, own, across, out, both):
    for i in range(4):
        both[i] = own[i]
        both[4 + i] = across[i]
        out[1 + i] = (mine[i] + theirs[i].astype(F32)).astype(BF16)
    is_odd = jnp.broadcast_to(odd[...], (BS, C)) > 0
    is_end = jnp.broadcast_to(end[...], (BS, C)) > 0
    third = jnp.where(is_end, edge[0], theirs[4])
    out[0] = jnp.where(is_odd, third, other[0])
    out[5] = jnp.where(is_odd, other[3], third)


def mix(dst, at, blocks, weight):
    rows = jnp.concatenate(blocks, axis=0)
    got = dot(rows, weight).astype(BF16)
    for j in range(len(blocks)):
        dst[at + j] = got[j * BS : (j + 1) * BS]


def mix_all(dst, own, weight):
    for g in range(4):
        mix(dst, 4 * g, own(g), weight)


def mix_absent(absent, dst, own, weight):
    @pl.when(absent)
    def _():
        mix_all(dst, own, weight)


def wide(node, level, columns):
    return jnp.concatenate([node[level, k] for k in columns], axis=1)


def near_pair(tab, at, i, mixed, nodes, columns):
    cols = []
    for k in columns:
        m = mixed[k]
        cols.append(jnp.concatenate([m[tab[at + 3 * i + k]], m[tab[at + 3 * i + 3 + k]]], axis=1))
    return dot(nodes, jnp.concatenate(cols, axis=0))


def sides(odd, first, second):
    is_odd = jnp.broadcast_to(odd[...], (BS, C)) > 0
    pick = lambda a, b: [jnp.where(is_odd, a[j], b[j]) for j in range(4)]
    return pick(first, second), pick(second, first)


def fine_body(table, odd, v0, first, second, node, chan, skip, out, m0, m1, m2, tab, sem):
    copy = pltpu.make_async_copy(table, tab, sem)
    copy.start()
    own = lambda g: [v0[4 * g + j] for j in range(4)]
    mix_all(m0, own, chan[0, 0])
    before, after = sides(odd, first, second)
    mix(m1, 0, before, chan[0, 1])
    mix(m2, 0, after, chan[0, 2])
    copy.wait()
    mix_absent(tab[LOW0] == 0, m1, own, chan[0, 1])
    mix_absent(tab[HIGH0] == 0, m2, own, chan[0, 2])
    nodes = wide(node, 0, range(KN))
    for i in range(0, BLK, 2):
        near = near_pair(tab, POS0, i, (m0, m1, m2), nodes, range(KN))
        skipped = dot(jnp.concatenate([v0[i], v0[i + 1]], axis=0), skip[...])
        out[i] = near[:, :C] + skipped[:BS]
        out[i + 1] = near[:, C:] + skipped[BS:]


def quad_parts(both, core):
    return lambda d: [(core if d % 2 else both)[4 * (d // 2) + j] for j in range(4)]


def own_body(table, both, core, all2, node, chan, n1, n2, a0, b0, tab, sem):
    copy = pltpu.make_async_copy(table, tab, sem)
    copy.start()
    mix_all(b0, lambda g: [all2[g, 1 + j] for j in range(4)], chan[2, 0])
    mix_all(a0, quad_parts(both, core), chan[1, 0])
    copy.wait()
    for out, at, m, level in ((n2, POS2, b0, 2), (n1, POS1, a0, 1)):
        for i in range(0, BLK, 2):
            pair = jnp.concatenate([m[tab[at + 3 * i]], m[tab[at + 3 * i + 3]]], axis=1)
            near = dot(node[level, 0], pair)
            out[i] = near[:, :C]
            out[i + 1] = near[:, C:]


def upward_body(
    table, odd, both, core, all2, first, second, node, chan, interp, acc0, n1, n2, out, a1, a2, b1, b2, c1, c2, tab, sem
):
    copy = pltpu.make_async_copy(table, tab, sem)
    copy.start()
    before, after = sides(odd, first, second)
    mix(b1, 0, before, chan[2, 1])
    mix(b2, 0, after, chan[2, 2])
    mix(a1, 0, [all2[j, 5] for j in range(4)], chan[1, 1])
    mix(a2, 0, [all2[j, 0] for j in range(4)], chan[1, 2])
    copy.wait()
    own2 = lambda g: [all2[g, 1 + j] for j in range(4)]
    own1 = quad_parts(both, core)
    mix_absent(tab[LOW2] == 0, b1, own2, chan[2, 1])
    mix_absent(tab[HIGH2] == 0, b2, own2, chan[2, 2])
    mix_absent(tab[LOW1] == 0, a1, own1, chan[1, 1])
    mix_absent(tab[HIGH1] == 0, a2, own1, chan[1, 2])
    halves = (slice(0, C), slice(C, 2 * C))
    nodes2 = wide(node, 2, (1, 2))
    for i in range(0, BLK, 2):
        top = near_pair(tab, POS2, i, (None, b1, b2), nodes2, (1, 2))
        for h in range(2):
            c2[i + h] = (n2[i + h] + top[:, halves[h]]).astype(BF16)
    nodes1 = wide(node, 1, (1, 2))
    for i in range(0, BLK, 2):
        mid = near_pair(tab, POS1, i, (None, a1, a2), nodes1, (1, 2))
        for h in range(2):
            b = i + h
            c1[b] = (n1[b] + mid[:, halves[h]] + dot(interp[1, tab[PICK2 + b]], c2[b])).astype(BF16)
    for b in range(BLK):
        u0 = acc0[b] + dot(interp[0, tab[PICK1 + b]], c1[b])
        out[b] = jax.nn.gelu(u0).astype(BF16)


def slots_of(rows, shift):
    child = (rows // shift) % 4
    which = jnp.arange(4, dtype=I32)
    hit = child[:, :, None] == which[None, None, :]
    return jnp.sum(jnp.where(hit, which[None, :, None], 0), axis=1)


def chosen(slot, who):
    hit = who[None, :, None] == jnp.arange(4, dtype=I32)[None, None, :]
    return jnp.sum(jnp.where(hit, slot[:, None, :], 0), axis=2)


def places(rows, start, pitch, key=None):
    rel = rows - start
    inner = rel if key is None else ((rel % 4) ^ key) * 4 + rel // 4
    low = rel + pitch - (BLK - HALO)
    high = rel - pitch
    pos = jnp.where(rel < 0, low, jnp.where(rel >= BLK, high, inner))
    return jnp.clip(pos, 0, BLK - 1).reshape(-1)


def body(v, near_fine, near_mid, near_top, restrict_mid, restrict_top, node, chan, restrict_w, interp_w, skip):
    x, r, zl, c, y = (lax.axis_index(a) for a in AXES)
    nx, nr, nzl, nc, ny = (lax.axis_size(a) for a in AXES)
    q = zl * nc + c
    dom = (x * nr + r) * nzl * nc + q
    v0 = v.reshape(BLK, BS, C)
    quads = v0.reshape(4, 2, 2, BS, C)
    take = lax.dynamic_slice_in_dim
    member = lambda index: lax.dynamic_index_in_dim(quads, index, axis=2, keepdims=False)
    flip = [(0, 1), (1, 0)]

    gifts = lax.all_gather(member(1 - c), "c", axis=0)

    total = nx * nr * nzl * nc * ny
    start0 = (dom * ny + y) * BLK
    start1 = ((x * nr + r) * ny + y) * BLK
    start2 = (x * ny + y) * BLK
    rows1 = take(restrict_mid, start1, BLK, 0)
    raw = jnp.concatenate([rows1.reshape(-1), q[None]])
    four = (4, BS, C)
    kept, sent = call(functools.partial(pair_body, (ny * BLK).bit_length() - 1), [(four, F32), (four, BF16)], 16, 40)(
        raw, restrict_w, quads, gifts
    )
    crossed = lax.ppermute(sent, "zl", flip)
    restrict_top, rows1, _ = lax.optimization_barrier((restrict_top, rows1, sent))
    slot1 = slots_of(rows1, ny * BLK)
    slot2 = slots_of(take(restrict_top, start2, BLK, 0), ny * BLK)
    order = jnp.arange(4, dtype=I32)
    mine = lambda slot: lax.dynamic_index_in_dim(slot.reshape(4, 4, 4), q, axis=1, keepdims=False)
    device = (dom * ny + y, x * nr + r, x)
    ends = (total - 1, nx * nr - 1, nx - 1)
    flags = []
    for at, end in zip(device, ends):
        flags += [at > 0, at < end]
    chosen2 = call(choose_body, ((8, BS, C), BF16), 0, 16)(chosen(mine(slot2), r ^ order[:2]).reshape(-1), restrict_w)
    crossed, chosen2 = lax.optimization_barrier((crossed, chosen2))
    v1 = call(sum_body, (four, BF16), 0, 16)(kept, crossed)

    near_fine, near_mid, near_top, slot1, slot2, _ = lax.optimization_barrier(
        (near_fine, near_mid, near_top, slot1, slot2, v1)
    )
    tab = jnp.concatenate(
        [
            chosen(slot1, q[None]).reshape(-1),
            chosen(slot2, r[None]).reshape(-1),
            places(near_fine, start0, BLK),
            places(take(near_mid, start1, BLK, 0), start1, ny * BLK, q),
            places(take(near_top, start2, BLK, 0), start2, ny * BLK, 0),
            jnp.stack(flags).astype(I32),
            jnp.zeros((TABLE - FLAG - 6,), I32),
        ]
    )

    other = lax.ppermute(v1, "r", [(j, j ^ 1) for j in range(nr)])
    across = lax.ppermute(v1, "zl", flip)

    odd = jnp.full((1, C), r % 2, F32)
    end = jnp.full((1, C), (r == 0) | (r == nr - 1), F32)
    other, tab = lax.optimization_barrier((other, tab))
    half, send = call(half_body, [(four, F32), ((5, BS, C), BF16)], 8, 32)(
        odd, chosen2, v1, other
    )
    theirs = lax.ppermute(send, "r", [(j, nr - 1 - j) for j in range(nr)])
    late1, _ = lax.optimization_barrier((v1, send))
    hop = [(nr * (i + 1) - 1, nr * (i + 1)) for i in range(nx - 1)]
    edge = lax.ppermute(
        jnp.where(r == 0, late1[:1], late1[3:]), ("x", "r"), hop + [(j, i) for i, j in hop]
    )
    ends0, _ = lax.optimization_barrier((v0, v1))
    odd_y = y % 2 == 1

    def pairs(count, begin):
        there = [(i, i + 1) for i in range(begin, count - 1, 2)]
        return there + [(j, i) for i, j in there]

    def end_blocks(first):
        return take(ends0, jnp.where(first, 0, BLK - HALO), HALO, 0)

    halo_a = lax.ppermute(end_blocks(odd_y), AXES, pairs(total, 0))
    halo_b = lax.ppermute(end_blocks(~odd_y), AXES, pairs(total, 1))

    part2, both = call(join_body, [((6, BS, C), BF16), ((8, BS, C), BF16)], 0, 34)(
        odd, end, half, theirs, other, edge, v1, across
    )
    all2 = lax.all_gather(part2, QUAD, axis=0, tiled=True).reshape(4, 6, BS, C)

    core = lax.ppermute(both, "c", flip)
    odd_x = x % 2 == 1

    def end_parents(first):
        return lax.dynamic_index_in_dim(all2, jnp.where(first, 1, 4), axis=1, keepdims=False)

    side_a = lax.ppermute(end_parents(odd_x), "x", pairs(nx, 0))
    side_b = lax.ppermute(end_parents(~odd_x), "x", pairs(nx, 1))

    mixed = pltpu.VMEM((BLK, BS, C), BF16)
    acc0 = call(fine_body, (v0.shape, F32), 88, 120, [mixed] * 3, 12)(
        tab, jnp.full((1, C), odd_y, F32), v0, halo_a, halo_b, node, chan, skip
    )
    n1, n2 = call(own_body, [(v0.shape, F32)] * 2, 64, 120, [mixed] * 2, 12)(
        tab, both, core, all2, node, chan
    )
    out = call(upward_body, (v0.shape, BF16), 112, 150, [mixed] * 6, 16)(
        tab, jnp.full((1, C), odd_x, F32), both, core, all2, side_a, side_b, node, chan, interp_w, acc0, n1, n2
    )
    return out.reshape(BLK * BS, C)


def solution(mesh):
    dom, sub = (mesh.shape[a] for a in ("dom", "sub"))
    grid = Mesh(mesh.devices.reshape(dom // 16, 4, 2, 2, sub), AXES)
    split = P(AXES, None)
    specs = (split, split) + (P(),) * 9
    return jax.shard_map(body, mesh=grid, in_specs=specs, out_specs=split, check_vma=False)
```

```python
import functools

import jax
import jax.numpy as jnp
from jax import lax
from jax.experimental import pallas as pl
from jax.experimental.pallas import tpu as pltpu
from jax.sharding import Mesh, PartitionSpec as P


C = 128
BS = 128
KN = 3
BLK = 16
HALO = 4
F32 = jnp.float32
BF16 = jnp.bfloat16
I32 = jnp.int32
AXES = ("x", "r", "zl", "c", "y")
QUAD = ("zl", "c")

VMEM = pl.BlockSpec(memory_space=pltpu.VMEM)
SMEM = pl.BlockSpec(memory_space=pltpu.SMEM)
ANY = pl.BlockSpec(memory_space=pl.ANY)

PICK1, PICK2, POS0, POS1, POS2, FLAG = 0, 16, 32, 80, 128, 176
LOW0, HIGH0, LOW1, HIGH1, LOW2, HIGH2 = range(FLAG, FLAG + 6)
TABLE = 256


def dot(a, b):
    return jnp.dot(a, b, preferred_element_type=F32)


def call(body, outs, products, blocks, scratch=None, limit=4, leaves=False):
    many = isinstance(outs, list)
    made = [jax.ShapeDtypeStruct(*o) for o in (outs if many else [outs])]

    def run(*args):
        return pl.pallas_call(
            body,
            out_shape=made if many else made[0],
            in_specs=[VMEM if a.dtype != I32 else SMEM if scratch is None else ANY for a in args],
            out_specs=[VMEM] * len(made) if many else ANY if leaves else VMEM,
            scratch_shapes=[] if scratch is None else [*scratch, pltpu.SMEM((TABLE,), I32), pltpu.SemaphoreType.DMA],
            cost_estimate=pl.CostEstimate(
                flops=products * 2 * BS * BS * C, bytes_accessed=blocks * BS * C * 2, transcendentals=0
            ),
            compiler_params=pltpu.CompilerParams(vmem_limit_bytes=limit << 20),
        )(*args)

    return run


def pair_body(shift, raw, w, own, gifts, keep, send):
    q = raw[4 * BLK]
    zl, c = q // 2, q % 2

    def slot(b, child):
        got = 0
        for t in range(1, 4):
            kid = jnp.bitwise_and(jnp.right_shift(raw[4 * b + t], shift), 3)
            got = got + jnp.where(kid == child, t, 0)
        return got

    for out, z in ((send, 1 - zl), (keep, zl)):
        for i in range(4):
            b = 4 * i + 2 * z + c
            acc = dot(w[0, slot(b, q)], own[i, z, c]) + dot(w[0, slot(b, jnp.bitwise_xor(q, 1))], gifts[1 - c, i, z])
            out[i] = acc.astype(out.dtype)


def sum_body(keep, got, out):
    for i in range(4):
        out[i] = (keep[i] + got[i].astype(F32)).astype(BF16)


def choose_body(slot, w, chosen):
    for i in range(8):
        chosen[i] = w[1, slot[i]]


def half_body(odd, chosen, own, other, keep, send):
    for i in range(4):
        acc = dot(chosen[2 * i], own[i]) + dot(chosen[2 * i + 1], other[i])
        keep[i] = acc
        send[i] = acc.astype(BF16)
    send[4] = jnp.where(jnp.broadcast_to(odd[...], (BS, C)) > 0, own[3], own[0])


def join_body(odd, end, mine, theirs, other, edge, own, across, out, both):
    for i in range(4):
        both[i] = own[i]
        both[4 + i] = across[i]
        out[1 + i] = (mine[i] + theirs[i].astype(F32)).astype(BF16)
    is_odd = jnp.broadcast_to(odd[...], (BS, C)) > 0
    is_end = jnp.broadcast_to(end[...], (BS, C)) > 0
    third = jnp.where(is_end, edge[0], theirs[4])
    out[0] = jnp.where(is_odd, third, other[0])
    out[5] = jnp.where(is_odd, other[3], third)


def mix(dst, at, blocks, weight):
    rows = jnp.concatenate(blocks, axis=0)
    got = dot(rows, weight).astype(BF16)
    for j in range(len(blocks)):
        dst[at + j] = got[j * BS : (j + 1) * BS]


def mix_all(dst, own, weight):
    for g in range(4):
        mix(dst, 4 * g, own(g), weight)


def mix_absent(absent, dst, own, weight):
    @pl.when(absent)
    def _():
        mix_all(dst, own, weight)


def wide(node, level, columns):
    return jnp.concatenate([node[level, k] for k in columns], axis=1)


def near_pair(tab, at, i, mixed, nodes, columns):
    cols = []
    for k in columns:
        m = mixed[k]
        cols.append(jnp.concatenate([m[tab[at + 3 * i + k]], m[tab[at + 3 * i + 3 + k]]], axis=1))
    return dot(nodes, jnp.concatenate(cols, axis=0))


def sides(odd, first, second):
    is_odd = jnp.broadcast_to(odd[...], (BS, C)) > 0
    pick = lambda a, b: [jnp.where(is_odd, a[j], b[j]) for j in range(4)]
    return pick(first, second), pick(second, first)


def fine_body(table, odd, v0, first, second, node, chan, skip, out, m0, m1, m2, tab, sem):
    copy = pltpu.make_async_copy(table, tab, sem)
    copy.start()
    own = lambda g: [v0[4 * g + j] for j in range(4)]
    mix_all(m0, own, chan[0, 0])
    before, after = sides(odd, first, second)
    mix(m1, 0, before, chan[0, 1])
    mix(m2, 0, after, chan[0, 2])
    copy.wait()
    mix_absent(tab[LOW0] == 0, m1, own, chan[0, 1])
    mix_absent(tab[HIGH0] == 0, m2, own, chan[0, 2])
    nodes = wide(node, 0, range(KN))
    for i in range(0, BLK, 2):
        near = near_pair(tab, POS0, i, (m0, m1, m2), nodes, range(KN))
        skipped = dot(jnp.concatenate([v0[i], v0[i + 1]], axis=0), skip[...])
        out[i] = near[:, :C] + skipped[:BS]
        out[i + 1] = near[:, C:] + skipped[BS:]


def quad_parts(both, core):
    return lambda d: [(core if d % 2 else both)[4 * (d // 2) + j] for j in range(4)]


def own_body(table, both, core, all2, node, chan, n1, n2, a0, b0, tab, sem):
    copy = pltpu.make_async_copy(table, tab, sem)
    copy.start()
    mix_all(b0, lambda g: [all2[g, 1 + j] for j in range(4)], chan[2, 0])
    mix_all(a0, quad_parts(both, core), chan[1, 0])
    copy.wait()
    for out, at, m, level in ((n2, POS2, b0, 2), (n1, POS1, a0, 1)):
        for i in range(0, BLK, 2):
            pair = jnp.concatenate([m[tab[at + 3 * i]], m[tab[at + 3 * i + 3]]], axis=1)
            near = dot(node[level, 0], pair)
            out[i] = near[:, :C]
            out[i + 1] = near[:, C:]


def upward_body(
    table, odd, both, core, all2, first, second, node, chan, interp, acc0, n1, n2, result, a1, a2, b1, b2, c1, c2, out, leave, tab, sem
):
    copy = pltpu.make_async_copy(table, tab, sem)
    copy.start()
    before, after = sides(odd, first, second)
    mix(b1, 0, before, chan[2, 1])
    mix(b2, 0, after, chan[2, 2])
    mix(a1, 0, [all2[j, 5] for j in range(4)], chan[1, 1])
    mix(a2, 0, [all2[j, 0] for j in range(4)], chan[1, 2])
    copy.wait()
    own2 = lambda g: [all2[g, 1 + j] for j in range(4)]
    own1 = quad_parts(both, core)
    mix_absent(tab[LOW2] == 0, b1, own2, chan[2, 1])
    mix_absent(tab[HIGH2] == 0, b2, own2, chan[2, 2])
    mix_absent(tab[LOW1] == 0, a1, own1, chan[1, 1])
    mix_absent(tab[HIGH1] == 0, a2, own1, chan[1, 2])
    halves = (slice(0, C), slice(C, 2 * C))
    nodes2 = wide(node, 2, (1, 2))
    for i in range(0, BLK, 2):
        top = near_pair(tab, POS2, i, (None, b1, b2), nodes2, (1, 2))
        for h in range(2):
            c2[i + h] = (n2[i + h] + top[:, halves[h]]).astype(BF16)
    nodes1 = wide(node, 1, (1, 2))
    for i in range(0, BLK, 2):
        mid = near_pair(tab, POS1, i, (None, a1, a2), nodes1, (1, 2))
        for h in range(2):
            b = i + h
            c1[b] = (n1[b] + mid[:, halves[h]] + dot(interp[1, tab[PICK2 + b]], c2[b])).astype(BF16)
    spans = [pl.ds(4 * g, 4) for g in range(4)]
    parts = [pltpu.make_async_copy(out.at[w], result.at[w], leave.at[g]) for g, w in enumerate(spans)]
    for b in range(BLK):
        u0 = acc0[b] + dot(interp[0, tab[PICK1 + b]], c1[b])
        out[b] = jax.nn.gelu(u0).astype(BF16)
        if b % 4 == 3 and b > 3:
            parts[b // 4 - 1].start()
    parts[3].start()
    for part in parts:
        part.wait()


def slots_of(rows, shift):
    child = (rows // shift) % 4
    which = jnp.arange(4, dtype=I32)
    hit = child[:, :, None] == which[None, None, :]
    return jnp.sum(jnp.where(hit, which[None, :, None], 0), axis=1)


def chosen(slot, who):
    hit = who[None, :, None] == jnp.arange(4, dtype=I32)[None, None, :]
    return jnp.sum(jnp.where(hit, slot[:, None, :], 0), axis=2)


def places(rows, start, pitch, key=None):
    rel = rows - start
    inner = rel if key is None else ((rel % 4) ^ key) * 4 + rel // 4
    low = rel + pitch - (BLK - HALO)
    high = rel - pitch
    pos = jnp.where(rel < 0, low, jnp.where(rel >= BLK, high, inner))
    return jnp.clip(pos, 0, BLK - 1).reshape(-1)


def body(v, near_fine, near_mid, near_top, restrict_mid, restrict_top, node, chan, restrict_w, interp_w, skip):
    x, r, zl, c, y = (lax.axis_index(a) for a in AXES)
    nx, nr, nzl, nc, ny = (lax.axis_size(a) for a in AXES)
    q = zl * nc + c
    dom = (x * nr + r) * nzl * nc + q
    v0 = v.reshape(BLK, BS, C)
    quads = v0.reshape(4, 2, 2, BS, C)
    take = lax.dynamic_slice_in_dim
    member = lambda index: lax.dynamic_index_in_dim(quads, index, axis=2, keepdims=False)
    flip = [(0, 1), (1, 0)]

    gift = member(1 - c)
    gifts = lax.all_gather(gift, "c", axis=0)

    total = nx * nr * nzl * nc * ny
    start0 = (dom * ny + y) * BLK
    start1 = ((x * nr + r) * ny + y) * BLK
    start2 = (x * ny + y) * BLK
    rows1 = take(restrict_mid, start1, BLK, 0)
    raw = jnp.concatenate([rows1.reshape(-1), q[None]])
    four = (4, BS, C)
    kept, sent = call(functools.partial(pair_body, (ny * BLK).bit_length() - 1), [(four, F32), (four, BF16)], 16, 40)(
        raw, restrict_w, quads, gifts
    )
    crossed = lax.ppermute(sent, "zl", flip)
    near_fine, near_mid, near_top, restrict_top, rows1, _ = lax.optimization_barrier(
        (near_fine, near_mid, near_top, restrict_top, rows1, sent)
    )
    slot1 = slots_of(rows1, ny * BLK)
    slot2 = slots_of(take(restrict_top, start2, BLK, 0), ny * BLK)
    order = jnp.arange(4, dtype=I32)
    mine = lambda slot: lax.dynamic_index_in_dim(slot.reshape(4, 4, 4), q, axis=1, keepdims=False)
    device = (dom * ny + y, x * nr + r, x)
    ends = (total - 1, nx * nr - 1, nx - 1)
    flags = []
    for at, end in zip(device, ends):
        flags += [at > 0, at < end]
    tab = jnp.concatenate(
        [
            chosen(slot1, q[None]).reshape(-1),
            chosen(slot2, r[None]).reshape(-1),
            places(near_fine, start0, BLK),
            places(take(near_mid, start1, BLK, 0), start1, ny * BLK, q),
            places(take(near_top, start2, BLK, 0), start2, ny * BLK, 0),
            jnp.stack(flags).astype(I32),
            jnp.zeros((TABLE - FLAG - 6,), I32),
        ]
    )

    chosen2 = call(choose_body, ((8, BS, C), BF16), 0, 16)(chosen(mine(slot2), r ^ order[:2]).reshape(-1), restrict_w)
    crossed, chosen2, tab = lax.optimization_barrier((crossed, chosen2, tab))
    v1 = call(sum_body, (four, BF16), 0, 16)(kept, crossed)

    other = lax.ppermute(v1, "r", [(j, j ^ 1) for j in range(nr)])
    across = lax.ppermute(v1, "zl", flip)

    odd = jnp.full((1, C), r % 2, F32)
    end = jnp.full((1, C), (r == 0) | (r == nr - 1), F32)
    half, send = call(half_body, [(four, F32), ((5, BS, C), BF16)], 8, 32)(
        odd, chosen2, v1, other
    )
    theirs = lax.ppermute(send, "r", [(j, nr - 1 - j) for j in range(nr)])
    late1, _ = lax.optimization_barrier((v1, send))
    hop = [(nr * (i + 1) - 1, nr * (i + 1)) for i in range(nx - 1)]
    edge = lax.ppermute(
        jnp.where(r == 0, late1[:1], late1[3:]), ("x", "r"), hop + [(j, i) for i, j in hop]
    )
    ends0, _ = lax.optimization_barrier((v0, v1))
    odd_y = y % 2 == 1

    def pairs(count, begin):
        there = [(i, i + 1) for i in range(begin, count - 1, 2)]
        return there + [(j, i) for i, j in there]

    def end_blocks(first):
        return take(ends0, jnp.where(first, 0, BLK - HALO), HALO, 0)

    halo_a = lax.ppermute(end_blocks(odd_y), AXES, pairs(total, 0))
    halo_b = lax.ppermute(end_blocks(~odd_y), AXES, pairs(total, 1))

    part2, both = call(join_body, [((6, BS, C), BF16), ((8, BS, C), BF16)], 0, 34)(
        odd, end, half, theirs, other, edge, v1, across
    )
    all2 = lax.all_gather(part2, QUAD, axis=0, tiled=True).reshape(4, 6, BS, C)

    core = lax.ppermute(both, "c", flip)
    odd_x = x % 2 == 1

    def end_parents(first):
        return lax.dynamic_index_in_dim(all2, jnp.where(first, 1, 4), axis=1, keepdims=False)

    side_a = lax.ppermute(end_parents(odd_x), "x", pairs(nx, 0))
    side_b = lax.ppermute(end_parents(~odd_x), "x", pairs(nx, 1))

    mixed = pltpu.VMEM((BLK, BS, C), BF16)
    acc0 = call(fine_body, (v0.shape, F32), 88, 120, [mixed] * 3, 12)(
        tab, jnp.full((1, C), odd_y, F32), v0, halo_a, halo_b, node, chan, skip
    )
    n1, n2 = call(own_body, [(v0.shape, F32)] * 2, 64, 120, [mixed] * 2, 12)(
        tab, both, core, all2, node, chan
    )
    out = call(upward_body, (v0.shape, BF16), 112, 150, [mixed] * 7 + [pltpu.SemaphoreType.DMA((4,))], 16, True)(
        tab, jnp.full((1, C), odd_x, F32), both, core, all2, side_a, side_b, node, chan, interp_w, acc0, n1, n2
    )
    return out.reshape(BLK * BS, C)


def solution(mesh):
    dom, sub = (mesh.shape[a] for a in ("dom", "sub"))
    grid = Mesh(mesh.devices.reshape(dom // 16, 4, 2, 2, sub), AXES)
    split = P(AXES, None)
    specs = (split, split) + (P(),) * 9
    return jax.shard_map(body, mesh=grid, in_specs=specs, out_specs=split, check_vma=False)
```
